256 devices in a mesh: acq: 32 (over z, x), rows: 8 (over y, core).
Axes of the slice: x: 4, y: 4, z: 8, core: 2. Of those that a mesh axis runs over, the one named last changes fastest.
Arguments:
- slc: bfloat16 [2, 32, 640, 5120], P(None, 'acq', 'rows'), may hold values from -600 to 600, as said below
- validity: int32 [32, 10], P('acq'), may hold values 0 or 1
Outputs:
- coherence: float32 [2, 128, 256, 320], P(None, None, ('acq', 'rows'))
The draws below stay inside these ranges and needn't reach their ends.
Inputs may be any that keep to these rules, and one draw needn't show every extreme that they name: `slc`: finite values.
All inputs are finite; a program needn't handle non-finite values. No bound on the sum of `validity` on one device may be relied on, other than what follows from the above.
Results may differ from the reference program's by a relative error of at most 0.0003.
Values may be sent and summed in bfloat16 or wider, within the bound.
A program may use at most 128 MiB of HBM per device.

```python
import jax
import jax.numpy as jnp
from jax import lax

PARTNERS = 10
AZ_LOOKS = 5
RG_LOOKS = 20
ACQ = 32
ROWS = 640
COLS = 5120
LOOK_R = 128
LOOK_C = 256
PAIRS = 320


def draw_slc(key, part):
    common_key = jax.random.fold_in(key, 11)
    field_keys = jax.random.split(common_key, 3)
    common_re = jnp.clip(jax.random.normal(field_keys[0], (ROWS, COLS), jnp.float32), -5.0, 5.0)
    common_im = jnp.clip(jax.random.normal(field_keys[1], (ROWS, COLS), jnp.float32), -5.0, 5.0)
    amplitude = jnp.exp(jax.random.uniform(field_keys[2], (ROWS, COLS), jnp.float32, jnp.log(0.5), jnp.log(2.0)))

    def single(index):
        acq_key = jax.random.fold_in(jax.random.fold_in(key, 23), index)
        parts = jax.random.split(acq_key, 4)
        sigma = jnp.exp(jax.random.uniform(parts[0], (), jnp.float32, jnp.log(0.3), jnp.log(3.0)))
        theta = jax.random.uniform(parts[1], (), jnp.float32, -jnp.pi, jnp.pi)
        noise_re = jnp.clip(jax.random.normal(parts[2], (ROWS, COLS), jnp.float32), -5.0, 5.0)
        noise_im = jnp.clip(jax.random.normal(parts[3], (ROWS, COLS), jnp.float32), -5.0, 5.0)
        base_re = amplitude * (common_re + sigma * noise_re)
        base_im = amplitude * (common_im + sigma * noise_im)
        rotated_re = jnp.cos(theta) * base_re - jnp.sin(theta) * base_im
        rotated_im = jnp.sin(theta) * base_re + jnp.cos(theta) * base_im
        return jnp.stack([rotated_re, rotated_im]).astype(jnp.bfloat16)
    stacked = lax.map(single, jnp.arange(ACQ, dtype=jnp.int32))
    return stacked.transpose(1, 0, 2, 3)


def set_ends(entries, stream_key, smallest, top_value):
    place = [jax.random.randint(jax.random.fold_in(stream_key, axis), (), 0, length) for axis, length in enumerate(entries.shape)]
    widest = entries.shape.index(max(entries.shape))
    next_to = place[:widest] + [(place[widest] + 1) % entries.shape[widest]] + place[widest + 1:]
    return entries.at[tuple(place)].set(smallest).at[tuple(next_to)].set(top_value)


def setup_inputs(seed: int = 0) -> dict:
    key_list = jax.random.split(jax.random.key(seed), 3)
    return {
        "slc": draw_slc(jax.random.fold_in(key_list[2], 71), 0),
        "validity": set_ends((jax.random.randint(key_list[1], (ACQ, PARTNERS), 0, 4) < 3).astype(jnp.int32), jax.random.fold_in(key_list[1], 1), 0, 1),
    }


EPS = 1e-06

def box_mean(values):
    count, rows, cols = values.shape
    shaped = values.reshape(count, rows // AZ_LOOKS, AZ_LOOKS, cols // RG_LOOKS, RG_LOOKS)
    return shaped.sum(axis=(2, 4)) / (AZ_LOOKS * RG_LOOKS)

def reference(slc, validity):
    padded = jnp.concatenate([slc, jnp.zeros((2, PARTNERS, ROWS, COLS), slc.dtype)], axis=1)
    offsets = jnp.arange(1, PARTNERS + 1, dtype=jnp.int32)

    def single(index):
        window = lax.dynamic_slice_in_dim(padded, index, PARTNERS + 1, 1).astype(jnp.float32)
        real_part = window[0]
        imag_part = window[1]
        power = box_mean(real_part * real_part + imag_part * imag_part)
        cross_re = real_part[:1] * real_part[1:] + imag_part[:1] * imag_part[1:]
        cross_im = imag_part[:1] * real_part[1:] - real_part[:1] * imag_part[1:]
        scale = lax.rsqrt((power[:1] + EPS) * (power[1:] + EPS))
        allowed = ((validity[index] > 0) & (index + offsets < ACQ)).astype(jnp.float32)[:, None, None]
        return jnp.stack([box_mean(cross_re) * scale * allowed, box_mean(cross_im) * scale * allowed])
    result = lax.map(single, jnp.arange(ACQ, dtype=jnp.int32))
    return result.transpose(1, 3, 4, 0, 2).reshape(2, LOOK_R, LOOK_C, PAIRS)
```

```python
import jax
import jax.numpy as jnp
from jax import lax
from jax.sharding import PartitionSpec as P
from jax.experimental import pallas as pl
from jax.experimental.pallas import tpu as pltpu

PARTNERS = 10
EPS = 1e-06
CELLS = 100.0
ACQ = 32
NX = 4
NZ = 8
BLOCK = 640
SLAB = 200
POWER_AT = ACQ * PARTNERS
SUMS = 384
MESH = pl.DeviceIdType.MESH
F32 = jnp.float32
BF16 = jnp.bfloat16


def z_offset(step):
    half = (step + 1) // 2
    return jnp.where(step % 2 == 1, half, lax.rem(NZ - half, NZ))


def z_position(offset):
    return jnp.where(offset <= 4, jnp.maximum(2 * offset - 1, 0), 2 * (NZ - offset))


def row_table():
    pieces = []
    for g in range(NX):
        q = lax.broadcasted_iota(jnp.int32, (40, 160), 0)
        take = ((q >> 2) & 1) * 80 + (4 * g + (q & 3)) * 5 + (q >> 3)
        pieces.append((lax.broadcasted_iota(jnp.int32, (40, 160), 1) == take).astype(F32))
    return jnp.concatenate(pieces, axis=0).astype(BF16)


def column_table():
    c = lax.broadcasted_iota(jnp.int32, (BLOCK, BLOCK), 1)
    take = (c & 31) * 20 + (c >> 7) * 4 + ((c >> 5) & 3)
    return (lax.broadcasted_iota(jnp.int32, (BLOCK, BLOCK), 0) == take).astype(F32).astype(BF16)


def kernel(
    slc_ref, validity_ref, out_ref,
    image, table, outgoing, arrived, lead, turned, sums, dense, message, received,
    own_valid, all_valid, power,
    in_sem, self_sem, send_sem, recv_sem, vsend_sem, vrecv_sem, send2_sem, recv2_sem,
):
    acq = lax.axis_index("acq")
    band = lax.axis_index("rows")
    z = acq // NX
    x = lax.rem(acq, NX)

    def z_at(step):
        return lax.rem(z + z_offset(step), NZ)

    def send_step(n):
        return lax.rem(n + 1, NZ)

    def load_block(n):
        at = pl.multiple_of(z_at(send_step(n)) * BLOCK, 128)
        return pltpu.make_async_copy(
            slc_ref.at[:, 0, :, pl.ds(at, BLOCK)], image.at[n], in_sem.at[n]
        )

    for n in range(NZ):
        load_block(n).start()

    barrier = pltpu.get_barrier_semaphore()

    def greet_acq(s, c):
        pl.semaphore_signal(
            barrier, inc=1, device_id=(lax.rem(acq + s, ACQ), band), device_id_type=MESH
        )
        return c

    lax.fori_loop(1, ACQ, greet_acq, 0)

    def greet_plane(s, c):
        pl.semaphore_signal(
            barrier,
            inc=1,
            device_id=(z * NX + s % NX, lax.rem(band + s // NX, 8)),
            device_id_type=MESH,
        )
        return c

    lax.fori_loop(NX, ACQ, greet_plane, 0)

    own_valid[...] = jnp.zeros_like(own_valid)
    own_valid[:, 0:PARTNERS] = (validity_ref[...] > 0).astype(F32)
    rows = row_table()
    table[...] = column_table()

    def prepare(n):
        load_block(n).wait()
        block = image[n].reshape(160, BLOCK)
        ordered = jnp.dot(rows, block, preferred_element_type=F32).astype(BF16)
        slab = jnp.dot(ordered, table[...], preferred_element_type=F32).astype(BF16)
        for g in range(NX):
            for c in range(5):
                outgoing[n, g, c * 40 : (c + 1) * 40, :] = slab[
                    g * 40 : (g + 1) * 40, c * 128 : (c + 1) * 128
                ]

    def slab_copy(n, g):
        return pltpu.make_async_remote_copy(
            src_ref=outgoing.at[n, g],
            dst_ref=arrived.at[acq],
            send_sem=send_sem.at[n, g],
            recv_sem=recv_sem.at[acq],
            device_id=(z_at(send_step(n)) * NX + g, band),
            device_id_type=MESH,
        )

    def valid_copy(to):
        return pltpu.make_async_remote_copy(
            src_ref=own_valid,
            dst_ref=all_valid.at[acq],
            send_sem=vsend_sem.at[to],
            recv_sem=vrecv_sem.at[acq],
            device_id=(to, band),
            device_id_type=MESH,
        )

    self_copy = pltpu.make_async_copy(outgoing.at[NZ - 1, x], arrived.at[acq], self_sem)

    def send(n):
        for g in range(NX):
            to = z_at(send_step(n)) * NX + g

            @pl.when(to != acq)
            def _():
                slab_copy(n, g).start()

    prepare(0)
    pl.semaphore_wait(barrier, 59)

    def prepare_and_send(n, c):
        send(n - 1)
        prepare(n)
        return c

    lax.fori_loop(1, NZ, prepare_and_send, 0)
    send(NZ - 1)
    self_copy.start()

    def send_valid(s, c):
        valid_copy(lax.rem(acq + s, ACQ)).start()
        return c

    lax.fori_loop(1, ACQ, send_valid, 0)

    for part in range(2):
        for k in range(1, PARTNERS + 1):
            sums[part, (k - 1) * ACQ + ACQ - k : k * ACQ] = jnp.zeros((k, 8, 128), F32)

    sublane = lax.broadcasted_iota(jnp.int32, (8, 128), 0)
    lane = lax.broadcasted_iota(jnp.int32, (8, 128), 1)
    upper = sublane < 4
    sign = jnp.where(upper, -1.0, 1.0).astype(F32)

    def slab_arrival(i):
        return pltpu.make_async_remote_copy(
            src_ref=outgoing.at[0, 0],
            dst_ref=arrived.at[i],
            send_sem=send_sem.at[0, 0],
            recv_sem=recv_sem.at[i],
            device_id=(acq, band),
            device_id_type=MESH,
        )

    def widen(i):
        for t in range(25):
            at = pl.ds(t * 8, 8)
            value = arrived[i, at, :].astype(F32)
            lead[i, at, :] = value
            turned[i, at, :] = pltpu.roll(value, 4, 0) * sign

    def pair_sums(za, gap):
        pairs = [
            (xa, xb)
            for xa in range(NX)
            for xb in range(NX)
            if 1 <= gap * NX + xb - xa <= PARTNERS
        ]
        powers = range(NX) if gap == 0 else ()

        def body(c, carry):
            carry = list(carry)
            for r in range(5):
                at = pl.ds(pl.multiple_of(c * 40 + r * 8, 8), 8)
                first = [lead[za * NX + i, at, :] for i in range(NX)]
                later = [lead[(za + gap) * NX + i, at, :] for i in range(NX)]
                later_turned = [turned[(za + gap) * NX + i, at, :] for i in range(NX)]
                m = 0
                for xa, xb in pairs:
                    carry[m] = carry[m] + first[xa] * later[xb]
                    carry[m + 1] = carry[m + 1] + first[xa] * later_turned[xb]
                    m += 2
                for i in powers:
                    carry[m] = carry[m] + first[i] * first[i]
                    m += 1
            return tuple(carry)

        zero = jnp.zeros((8, 128), F32)
        total = lax.fori_loop(0, 5, body, (zero,) * (2 * len(pairs) + len(powers)))
        m = 0
        for xa, xb in pairs:
            k = gap * NX + xb - xa
            slot = (k - 1) * ACQ + za * NX + xa
            sums[0, slot] = total[m]
            sums[1, slot] = total[m + 1]
            m += 2
        for i in powers:
            sums[0, POWER_AT + za * NX + i] = total[m]
            m += 1

    def arrival(step, carry):
        zn = z_at(step)
        for i in range(NX):
            source = zn * NX + i

            @pl.when(source != acq)
            def _():
                slab_arrival(source).wait_recv()

            @pl.when(source == acq)
            def _():
                self_copy.wait()

            widen(source)
        pair_sums(zn, 0)
        for gap in (1, 2, 3):

            def side(s, c):
                za = jnp.where(s == 0, zn - gap, zn)
                other = jnp.where(s == 0, zn - gap, zn + gap)
                place = z_position(lax.rem(other - z + 2 * NZ, NZ))

                @pl.when((other >= 0) & (other < NZ) & (place < step))
                def _():
                    pair_sums(za, gap)

                return c

            lax.fori_loop(0, 2, side, 0)
        return carry

    lax.fori_loop(0, NZ, arrival, 0)

    top_lane = (lane & 64) == 0
    mid_lane = (lane & 32) == 0
    s1 = (sublane & 2) == 0
    s0 = (sublane & 1) == 0

    def gather_group(part, group):
        v = [sums[part, group * 8 + i] for i in range(8)]

        def fold_part(a, b):
            return jnp.where(upper, a, b) + pltpu.roll(jnp.where(upper, b, a), 4, 0)

        v = [fold_part(v[i], v[i + 4]) for i in range(4)]

        def fold_top(a, b):
            return jnp.where(top_lane, a, b) + pltpu.roll(jnp.where(top_lane, b, a), 64, 1)

        v = [fold_top(v[i], v[i + 2]) for i in range(2)]
        a, b = v
        w = jnp.where(mid_lane, a + pltpu.roll(a, 96, 1), b + pltpu.roll(b, 32, 1))
        u = pltpu.roll(w, 64, 1)
        w = jnp.where(
            s1 == top_lane, w, jnp.where(s1, pltpu.roll(u, 6, 0), pltpu.roll(u, 2, 0))
        )
        w = jnp.where(
            s0 == mid_lane,
            w,
            jnp.where(
                s0,
                pltpu.roll(pltpu.roll(w, 32, 1), 7, 0),
                pltpu.roll(pltpu.roll(w, 96, 1), 1, 0),
            ),
        )
        dense[part, pl.ds(pl.multiple_of(group * 8, 8), 8), :] = w

    def gather_both(group, c):
        gather_group(0, group)
        gather_group(1, group)
        return c

    lax.fori_loop(0, 40, gather_both, 0)

    def gather_power(group, c):
        gather_group(0, group)
        return c

    lax.fori_loop(40, 44, gather_power, 0)

    for part in range(2):
        for h in range(3):
            flipped = dense[part, h * 128 : (h + 1) * 128, :].T
            for lr in range(4):
                message[h, pl.ds(part * 4 + lr, 32, stride=8), :] = flipped[
                    lr * 32 : (lr + 1) * 32, :
                ]

    own_look = x * 8 + band
    own_source = band * NX + x

    def message_copy(look):
        return pltpu.make_async_remote_copy(
            src_ref=message.at[:, pl.ds(pl.multiple_of(look * 8, 8), 8), :],
            dst_ref=received.at[own_source],
            send_sem=send2_sem.at[look],
            recv_sem=recv2_sem.at[own_source],
            device_id=(z * NX + look // 8, lax.rem(look, 8)),
            device_id_type=MESH,
        )

    def send_message(s, c):
        message_copy(lax.rem(own_look + s, ACQ)).start()
        return c

    lax.fori_loop(1, ACQ, send_message, 0)
    for h in range(3):
        received[own_source, h] = message[h, pl.ds(pl.multiple_of(own_look * 8, 8), 8), :]

    def valid_arrival(s, c):
        i = lax.rem(acq + s, ACQ)
        pltpu.make_async_remote_copy(
            src_ref=own_valid,
            dst_ref=all_valid.at[i],
            send_sem=vsend_sem.at[i],
            recv_sem=vrecv_sem.at[i],
            device_id=(i, band),
            device_id_type=MESH,
        ).wait()
        return c

    lax.fori_loop(1, ACQ, valid_arrival, 0)
    all_valid[acq] = own_valid[...]

    for n in range(NZ):
        for g in range(NX):

            @pl.when(z_at(send_step(n)) * NX + g != acq)
            def _():
                slab_copy(n, g).wait_send()

    def message_arrival(s, c):
        look = lax.rem(own_look + s, ACQ)
        message_copy(look).wait_send()
        source = lax.rem(own_source + s, ACQ)
        pltpu.make_async_remote_copy(
            src_ref=message.at[:, pl.ds(0, 8), :],
            dst_ref=received.at[source],
            send_sem=send2_sem.at[0],
            recv_sem=recv2_sem.at[source],
            device_id=(acq, band),
            device_id_type=MESH,
        ).wait_recv()
        return c

    lax.fori_loop(1, ACQ, message_arrival, 0)

    final = [[], []]
    for h in range(3):
        parts = [[], []]
        for s in range(0, ACQ, 2):
            a = received[s, h]
            b = received[s + 1, h]
            parts[0].append(jnp.where(upper, a, pltpu.roll(b, 4, 0)))
            parts[1].append(jnp.where(upper, pltpu.roll(a, 4, 0), b))
        for part in range(2):
            final[part].append(jnp.concatenate(parts[part], axis=0).T)

    power[...] = jnp.ones_like(power)
    power[0:ACQ, :] = final[0][2][64:96, :] * (1.0 / CELLS) + EPS
    valid = all_valid[...].reshape(ACQ, 128)
    position = lax.broadcasted_iota(jnp.int32, (ACQ, 128), 0)
    for k in range(1, PARTNERS + 1):
        scale = lax.rsqrt(power[0:ACQ, :] * power[k : k + ACQ, :]) * (1.0 / CELLS)
        on = jnp.broadcast_to(valid[:, k - 1 : k], (ACQ, 128))
        weight = jnp.where(position + k < ACQ, scale * on, 0.0)
        h, at = divmod((k - 1) * ACQ, 128)
        for part in range(2):
            out_ref[part, pl.ds(k - 1, ACQ, stride=PARTNERS), :] = (
                final[part][h][at : at + ACQ, :] * weight
            )


def per_device(slc, validity):
    dma = pltpu.SemaphoreType.DMA
    out = pl.pallas_call(
        kernel,
        out_shape=jax.ShapeDtypeStruct((2, ACQ * PARTNERS, 128), F32),
        in_specs=[
            pl.BlockSpec(memory_space=pl.ANY),
            pl.BlockSpec(memory_space=pltpu.VMEM),
        ],
        out_specs=pl.BlockSpec(memory_space=pltpu.VMEM),
        scratch_shapes=[
            pltpu.VMEM((NZ, 2, 80, BLOCK), BF16),
            pltpu.VMEM((BLOCK, BLOCK), BF16),
            pltpu.VMEM((NZ, NX, SLAB, 128), BF16),
            pltpu.VMEM((ACQ, SLAB, 128), BF16),
            pltpu.VMEM((ACQ, SLAB, 128), F32),
            pltpu.VMEM((ACQ, SLAB, 128), F32),
            pltpu.VMEM((2, SUMS, 8, 128), F32),
            pltpu.VMEM((2, SUMS, 128), F32),
            pltpu.VMEM((3, 256, 128), F32),
            pltpu.VMEM((ACQ, 3, 8, 128), F32),
            pltpu.VMEM((1, 128), F32),
            pltpu.VMEM((ACQ, 1, 128), F32),
            pltpu.VMEM((48, 128), F32),
            dma((NZ,)),
            dma,
            dma((NZ, NX)),
            dma((ACQ,)),
            dma((ACQ,)),
            dma((ACQ,)),
            dma((ACQ,)),
            dma((ACQ,)),
        ],
        compiler_params=pltpu.CompilerParams(
            collective_id=0, has_side_effects=True, vmem_limit_bytes=56 * 2**20
        ),
    )(slc, validity)
    return out.transpose(0, 2, 1)[:, :, None, :]


def solution(mesh):
    in_specs = (P(None, "acq", "rows", None), P("acq", None))
    out_specs = P(None, None, ("acq", "rows"), None)
    return jax.shard_map(
        per_device, mesh=mesh, in_specs=in_specs, out_specs=out_specs, check_vma=False
    )
```

```python
import jax
import jax.numpy as jnp
from jax import lax
from jax.sharding import PartitionSpec as P
from jax.experimental import pallas as pl
from jax.experimental.pallas import tpu as pltpu

PARTNERS = 10
EPS = 1e-06
CELLS = 100.0
ACQ = 32
NX = 4
NZ = 8
BLOCK = 640
SLAB = 200
POWER_AT = ACQ * PARTNERS
SUMS = 384
MESH = pl.DeviceIdType.MESH
F32 = jnp.float32
BF16 = jnp.bfloat16


def z_offset(step):
    half = (step + 1) // 2
    return jnp.where(step % 2 == 1, half, lax.rem(NZ - half, NZ))


def z_position(offset):
    return jnp.where(offset <= 4, jnp.maximum(2 * offset - 1, 0), 2 * (NZ - offset))


def row_table():
    pieces = []
    for g in range(NX):
        q = lax.broadcasted_iota(jnp.int32, (40, 160), 0)
        take = ((q >> 2) & 1) * 80 + (4 * g + (q & 3)) * 5 + (q >> 3)
        pieces.append((lax.broadcasted_iota(jnp.int32, (40, 160), 1) == take).astype(F32))
    return jnp.concatenate(pieces, axis=0).astype(BF16)


def column_table():
    c = lax.broadcasted_iota(jnp.int32, (BLOCK, BLOCK), 1)
    take = (c & 31) * 20 + (c >> 7) * 4 + ((c >> 5) & 3)
    return (lax.broadcasted_iota(jnp.int32, (BLOCK, BLOCK), 0) == take).astype(F32).astype(BF16)


def kernel(
    slc_ref, validity_ref, out_ref,
    image, table, outgoing, arrived, lead, turned, sums, dense, message, received,
    own_valid, all_valid, power,
    in_sem, self_sem, send_sem, recv_sem, vsend_sem, vrecv_sem, send2_sem, recv2_sem,
):
    acq = lax.axis_index("acq")
    band = lax.axis_index("rows")
    z = acq // NX
    x = lax.rem(acq, NX)

    def z_at(step):
        return lax.rem(z + z_offset(step), NZ)

    def send_step(n):
        return lax.rem(n + 1, NZ)

    def load_block(n):
        at = pl.multiple_of(z_at(send_step(n)) * BLOCK, 128)
        return pltpu.make_async_copy(
            slc_ref.at[:, 0, :, pl.ds(at, BLOCK)], image.at[n], in_sem.at[n]
        )

    for n in range(NZ):
        load_block(n).start()

    barrier = pltpu.get_barrier_semaphore()

    def greet_acq(s, c):
        pl.semaphore_signal(
            barrier, inc=1, device_id=(lax.rem(acq + s, ACQ), band), device_id_type=MESH
        )
        return c

    lax.fori_loop(1, ACQ, greet_acq, 0)

    def greet_plane(s, c):
        pl.semaphore_signal(
            barrier,
            inc=1,
            device_id=(z * NX + s % NX, lax.rem(band + s // NX, 8)),
            device_id_type=MESH,
        )
        return c

    lax.fori_loop(NX, ACQ, greet_plane, 0)

    own_valid[...] = jnp.zeros_like(own_valid)
    own_valid[:, 0:PARTNERS] = (validity_ref[...] > 0).astype(F32)
    rows = row_table()
    table[...] = column_table()

    def prepare(n):
        load_block(n).wait()
        block = image[n].reshape(160, BLOCK)
        ordered = jnp.dot(rows, block, preferred_element_type=F32).astype(BF16)
        slab = jnp.dot(ordered, table[...], preferred_element_type=F32).astype(BF16)
        for g in range(NX):
            for c in range(5):
                outgoing[n, g, c * 40 : (c + 1) * 40, :] = slab[
                    g * 40 : (g + 1) * 40, c * 128 : (c + 1) * 128
                ]

    def slab_copy(n, g):
        return pltpu.make_async_remote_copy(
            src_ref=outgoing.at[n, g],
            dst_ref=arrived.at[acq],
            send_sem=send_sem.at[n, g],
            recv_sem=recv_sem.at[acq],
            device_id=(z_at(send_step(n)) * NX + g, band),
            device_id_type=MESH,
        )

    def valid_copy(to):
        return pltpu.make_async_remote_copy(
            src_ref=own_valid,
            dst_ref=all_valid.at[acq],
            send_sem=vsend_sem.at[to],
            recv_sem=vrecv_sem.at[acq],
            device_id=(to, band),
            device_id_type=MESH,
        )

    self_copy = pltpu.make_async_copy(outgoing.at[NZ - 1, x], arrived.at[acq], self_sem)

    def send(n):
        for g in range(NX):
            to = z_at(send_step(n)) * NX + g

            @pl.when(to != acq)
            def _():
                slab_copy(n, g).start()

    prepare(0)
    pl.semaphore_wait(barrier, 59)

    def send_valid(s, c):
        valid_copy(lax.rem(acq + s, ACQ)).start()
        return c

    lax.fori_loop(1, ACQ, send_valid, 0)

    def prepare_and_send(n, c):
        send(n - 1)
        prepare(n)
        return c

    lax.fori_loop(1, NZ, prepare_and_send, 0)
    send(NZ - 1)
    self_copy.start()

    for part in range(2):
        for k in range(1, PARTNERS + 1):
            sums[part, (k - 1) * ACQ + ACQ - k : k * ACQ] = jnp.zeros((k, 8, 128), F32)

    sublane = lax.broadcasted_iota(jnp.int32, (8, 128), 0)
    lane = lax.broadcasted_iota(jnp.int32, (8, 128), 1)
    upper = sublane < 4
    sign = jnp.where(upper, -1.0, 1.0).astype(F32)

    def slab_arrival(i):
        return pltpu.make_async_remote_copy(
            src_ref=outgoing.at[0, 0],
            dst_ref=arrived.at[i],
            send_sem=send_sem.at[0, 0],
            recv_sem=recv_sem.at[i],
            device_id=(acq, band),
            device_id_type=MESH,
        )

    def valid_arrival(i):
        pltpu.make_async_remote_copy(
            src_ref=own_valid,
            dst_ref=all_valid.at[i],
            send_sem=vsend_sem.at[i],
            recv_sem=vrecv_sem.at[i],
            device_id=(i, band),
            device_id_type=MESH,
        ).wait()

    all_valid[acq] = own_valid[...]

    def widen(i):
        for t in range(25):
            at = pl.ds(t * 8, 8)
            value = arrived[i, at, :].astype(F32)
            lead[i, at, :] = value
            turned[i, at, :] = pltpu.roll(value, 4, 0) * sign

    def pair_sums(za, gap):
        pairs = [
            (xa, xb)
            for xa in range(NX)
            for xb in range(NX)
            if 1 <= gap * NX + xb - xa <= PARTNERS
        ]
        powers = range(NX) if gap == 0 else ()

        def body(c, carry):
            carry = list(carry)
            for r in range(5):
                at = pl.ds(pl.multiple_of(c * 40 + r * 8, 8), 8)
                first = [lead[za * NX + i, at, :] for i in range(NX)]
                later = [lead[(za + gap) * NX + i, at, :] for i in range(NX)]
                later_turned = [turned[(za + gap) * NX + i, at, :] for i in range(NX)]
                m = 0
                for xa, xb in pairs:
                    carry[m] = carry[m] + first[xa] * later[xb]
                    carry[m + 1] = carry[m + 1] + first[xa] * later_turned[xb]
                    m += 2
                for i in powers:
                    carry[m] = carry[m] + first[i] * first[i]
                    m += 1
            return tuple(carry)

        zero = jnp.zeros((8, 128), F32)
        total = lax.fori_loop(0, 5, body, (zero,) * (2 * len(pairs) + len(powers)))
        m = 0
        for xa, xb in pairs:
            k = gap * NX + xb - xa
            slot = (k - 1) * ACQ + za * NX + xa
            sums[0, slot] = total[m]
            sums[1, slot] = total[m + 1]
            m += 2
        for i in powers:
            sums[0, POWER_AT + za * NX + i] = total[m]
            m += 1

    def arrival(step, carry):
        zn = z_at(step)
        for i in range(NX):
            source = zn * NX + i

            @pl.when(source != acq)
            def _():
                valid_arrival(source)
                slab_arrival(source).wait_recv()

            @pl.when(source == acq)
            def _():
                self_copy.wait()

            widen(source)
        pair_sums(zn, 0)
        for gap in (1, 2, 3):

            def side(s, c):
                za = jnp.where(s == 0, zn - gap, zn)
                other = jnp.where(s == 0, zn - gap, zn + gap)
                place = z_position(lax.rem(other - z + 2 * NZ, NZ))

                @pl.when((other >= 0) & (other < NZ) & (place < step))
                def _():
                    pair_sums(za, gap)

                return c

            lax.fori_loop(0, 2, side, 0)
        return carry

    lax.fori_loop(0, NZ, arrival, 0)

    top_lane = (lane & 64) == 0
    mid_lane = (lane & 32) == 0
    s1 = (sublane & 2) == 0
    s0 = (sublane & 1) == 0

    def gather_group(part, group):
        v = [sums[part, group * 8 + i] for i in range(8)]

        def fold_part(a, b):
            return jnp.where(upper, a, b) + pltpu.roll(jnp.where(upper, b, a), 4, 0)

        v = [fold_part(v[i], v[i + 4]) for i in range(4)]

        def fold_top(a, b):
            return jnp.where(top_lane, a, b) + pltpu.roll(jnp.where(top_lane, b, a), 64, 1)

        v = [fold_top(v[i], v[i + 2]) for i in range(2)]
        a, b = v
        w = jnp.where(mid_lane, a + pltpu.roll(a, 96, 1), b + pltpu.roll(b, 32, 1))
        u = pltpu.roll(w, 64, 1)
        w = jnp.where(
            s1 == top_lane, w, jnp.where(s1, pltpu.roll(u, 6, 0), pltpu.roll(u, 2, 0))
        )
        w = jnp.where(
            s0 == mid_lane,
            w,
            jnp.where(
                s0,
                pltpu.roll(pltpu.roll(w, 32, 1), 7, 0),
                pltpu.roll(pltpu.roll(w, 96, 1), 1, 0),
            ),
        )
        return w

    def gather_batch(which):
        values = [gather_group(part, group) for part, group in which]
        for (part, group), value in zip(which, values):
            dense[part, pl.ds(pl.multiple_of(group * 8, 8), 8), :] = value

    def gather_both(batch, c):
        gather_batch([(part, batch * 5 + i) for part in range(2) for i in range(5)])
        return c

    lax.fori_loop(0, 8, gather_both, 0)
    gather_batch([(0, 40 + i) for i in range(4)])

    for part in range(2):
        for h in range(3):
            flipped = dense[part, h * 128 : (h + 1) * 128, :].T
            for lr in range(4):
                message[h, pl.ds(part * 4 + lr, 32, stride=8), :] = flipped[
                    lr * 32 : (lr + 1) * 32, :
                ]

    own_look = x * 8 + band
    own_source = band * NX + x

    def message_copy(look):
        return pltpu.make_async_remote_copy(
            src_ref=message.at[:, pl.ds(pl.multiple_of(look * 8, 8), 8), :],
            dst_ref=received.at[own_source],
            send_sem=send2_sem.at[look],
            recv_sem=recv2_sem.at[own_source],
            device_id=(z * NX + look // 8, lax.rem(look, 8)),
            device_id_type=MESH,
        )

    def send_message(s, c):
        message_copy(lax.rem(own_look + s, ACQ)).start()
        return c

    lax.fori_loop(1, ACQ, send_message, 0)
    for h in range(3):
        received[own_source, h] = message[h, pl.ds(pl.multiple_of(own_look * 8, 8), 8), :]

    for n in range(NZ):
        for g in range(NX):

            @pl.when(z_at(send_step(n)) * NX + g != acq)
            def _():
                slab_copy(n, g).wait_send()

    def message_arrival(s, c):
        look = lax.rem(own_look + s, ACQ)
        message_copy(look).wait_send()
        source = lax.rem(own_source + s, ACQ)
        pltpu.make_async_remote_copy(
            src_ref=message.at[:, pl.ds(0, 8), :],
            dst_ref=received.at[source],
            send_sem=send2_sem.at[0],
            recv_sem=recv2_sem.at[source],
            device_id=(acq, band),
            device_id_type=MESH,
        ).wait_recv()
        return c

    lax.fori_loop(1, ACQ, message_arrival, 0)

    final = [[], []]
    for h in range(3):
        parts = [[], []]
        for s in range(0, ACQ, 2):
            a = received[s, h]
            b = received[s + 1, h]
            parts[0].append(jnp.where(upper, a, pltpu.roll(b, 4, 0)))
            parts[1].append(jnp.where(upper, pltpu.roll(a, 4, 0), b))
        for part in range(2):
            final[part].append(jnp.concatenate(parts[part], axis=0).T)

    power[...] = jnp.ones_like(power)
    power[0:ACQ, :] = final[0][2][64:96, :] * (1.0 / CELLS) + EPS
    valid = all_valid[...].reshape(ACQ, 128)
    position = lax.broadcasted_iota(jnp.int32, (ACQ, 128), 0)
    for k in range(1, PARTNERS + 1):
        scale = lax.rsqrt(power[0:ACQ, :] * power[k : k + ACQ, :]) * (1.0 / CELLS)
        on = jnp.broadcast_to(valid[:, k - 1 : k], (ACQ, 128))
        weight = jnp.where(position + k < ACQ, scale * on, 0.0)
        h, at = divmod((k - 1) * ACQ, 128)
        for part in range(2):
            out_ref[part, pl.ds(k - 1, ACQ, stride=PARTNERS), :] = (
                final[part][h][at : at + ACQ, :] * weight
            )


def per_device(slc, validity):
    dma = pltpu.SemaphoreType.DMA
    out = pl.pallas_call(
        kernel,
        out_shape=jax.ShapeDtypeStruct((2, ACQ * PARTNERS, 128), F32),
        in_specs=[
            pl.BlockSpec(memory_space=pl.ANY),
            pl.BlockSpec(memory_space=pltpu.VMEM),
        ],
        out_specs=pl.BlockSpec(memory_space=pltpu.VMEM),
        scratch_shapes=[
            pltpu.VMEM((NZ, 2, 80, BLOCK), BF16),
            pltpu.VMEM((BLOCK, BLOCK), BF16),
            pltpu.VMEM((NZ, NX, SLAB, 128), BF16),
            pltpu.VMEM((ACQ, SLAB, 128), BF16),
            pltpu.VMEM((ACQ, SLAB, 128), F32),
            pltpu.VMEM((ACQ, SLAB, 128), F32),
            pltpu.VMEM((2, SUMS, 8, 128), F32),
            pltpu.VMEM((2, SUMS, 128), F32),
            pltpu.VMEM((3, 256, 128), F32),
            pltpu.VMEM((ACQ, 3, 8, 128), F32),
            pltpu.VMEM((1, 128), F32),
            pltpu.VMEM((ACQ, 1, 128), F32),
            pltpu.VMEM((48, 128), F32),
            dma((NZ,)),
            dma,
            dma((NZ, NX)),
            dma((ACQ,)),
            dma((ACQ,)),
            dma((ACQ,)),
            dma((ACQ,)),
            dma((ACQ,)),
        ],
        compiler_params=pltpu.CompilerParams(
            collective_id=0, has_side_effects=True, vmem_limit_bytes=56 * 2**20
        ),
    )(slc, validity)
    return out.transpose(0, 2, 1)[:, :, None, :]


def solution(mesh):
    in_specs = (P(None, "acq", "rows", None), P("acq", None))
    out_specs = P(None, None, ("acq", "rows"), None)
    return jax.shard_map(
        per_device, mesh=mesh, in_specs=in_specs, out_specs=out_specs, check_vma=False
    )
```

```python
import jax
import jax.numpy as jnp
from jax import lax
from jax.sharding import PartitionSpec as P
from jax.experimental import pallas as pl
from jax.experimental.pallas import tpu as pltpu

PARTNERS = 10
EPS = 1e-06
CELLS = 100.0
ACQ = 32
NX = 4
NZ = 8
BLOCK = 640
CUT = 160
SLAB = 200
PAIRS_Z = NX * PARTNERS
POWER_AT = 2 * PAIRS_Z
SUMS = 88
MESH = pl.DeviceIdType.MESH
F32 = jnp.float32
BF16 = jnp.bfloat16


def z_offset(step):
    half = (step + 1) // 2
    return jnp.where(step % 2 == 1, half, lax.rem(NZ - half, NZ))


def z_position(offset):
    return jnp.where(offset <= 4, jnp.maximum(2 * offset - 1, 0), 2 * (NZ - offset))


def row_table():
    pieces = []
    for g in range(NX):
        q = lax.broadcasted_iota(jnp.int32, (40, 160), 0)
        take = ((q >> 2) & 1) * 80 + (4 * g + (q & 3)) * 5 + (q >> 3)
        pieces.append((lax.broadcasted_iota(jnp.int32, (40, 160), 1) == take).astype(F32))
    return jnp.concatenate(pieces, axis=0).astype(BF16)


def column_table():
    c = lax.broadcasted_iota(jnp.int32, (BLOCK, BLOCK), 1)
    take = (c & 31) * 20 + (c >> 7) * 4 + ((c >> 5) & 3)
    return (lax.broadcasted_iota(jnp.int32, (BLOCK, BLOCK), 0) == take).astype(F32).astype(BF16)


def kernel(
    slc_ref, validity_ref, out_ref,
    image, table, outgoing, arrived, lead, turned, sums, dense, message, received,
    final, weight, own_valid, all_valid, power,
    z_sem, plane_sem, in_sem, self_sem, send_sem, recv_sem, last_sem, vsend_sem, vrecv_sem, send2_sem, recv2_sem,
):
    acq = lax.axis_index("acq")
    band = lax.axis_index("rows")
    z = acq // NX
    x = lax.rem(acq, NX)

    def z_at(step):
        return lax.rem(z + z_offset(step), NZ)

    def load_block(n):
        at = pl.multiple_of(z_at(n) * BLOCK, 128)
        return pltpu.make_async_copy(
            slc_ref.at[:, 0, :, pl.ds(at, BLOCK)], image.at[n], in_sem.at[n]
        )

    for n in range(NZ):
        load_block(n).start()

    barrier = pltpu.get_barrier_semaphore()
    along_z = [(lax.rem(z + d, NZ) * NX + x, band) for d in (1, NZ - 1)]
    along_x = [(z * NX + lax.rem(x + d, NX), band) for d in (1, 2, 3)]
    bands = [(acq, lax.rem(band + d, 8)) for d in (2, 6)]
    bands.append((acq, band + 1 - 2 * lax.rem(band, 2)))

    def tell(semaphore, devices):
        for device in devices:
            pl.semaphore_signal(semaphore, inc=1, device_id=device, device_id_type=MESH)

    tell(barrier, along_x + along_z + bands)

    own_valid[...] = jnp.zeros_like(own_valid)
    own_valid[:, 0:PARTNERS] = (validity_ref[...] > 0).astype(F32)
    rows = row_table()
    table[...] = column_table()

    def prepare(n):
        load_block(n).wait()
        block = image[n].reshape(160, BLOCK)
        ordered = jnp.dot(rows, block, preferred_element_type=F32).astype(BF16)
        slab = jnp.dot(ordered, table[...], preferred_element_type=F32).astype(BF16)
        for g in range(NX):
            for c in range(5):
                outgoing[n * NX + g, c * 40 : (c + 1) * 40, :] = slab[
                    g * 40 : (g + 1) * 40, c * 128 : (c + 1) * 128
                ]

    def slab_copy(n, g, at, recv):
        return pltpu.make_async_remote_copy(
            src_ref=outgoing.at[n * NX + g, at, :],
            dst_ref=arrived.at[acq, at, :],
            send_sem=send_sem,
            recv_sem=recv,
            device_id=(z_at(n) * NX + g, band),
            device_id_type=MESH,
        )

    whole = pl.ds(0, SLAB)
    first_rows = pl.ds(0, CUT)
    last_rows = pl.ds(CUT, SLAB - CUT)

    def valid_copy(to):
        return pltpu.make_async_remote_copy(
            src_ref=own_valid,
            dst_ref=all_valid.at[acq],
            send_sem=vsend_sem,
            recv_sem=vrecv_sem,
            device_id=(to, band),
            device_id_type=MESH,
        )

    self_copy = pltpu.make_async_copy(outgoing.at[x], arrived.at[acq], self_sem)

    def send(n):
        for g in range(NX):
            to = z_at(n) * NX + g

            @pl.when(to != acq)
            def _():
                valid_copy(to).start()
                slab_copy(n, g, whole, recv_sem.at[acq]).start()

    prepare(0)
    pl.semaphore_wait(barrier, 8)
    tell(z_sem.at[0], along_z)
    tell(plane_sem.at[0], bands)
    send(0)
    self_copy.start()

    def ring(d, c):
        pl.semaphore_wait(z_sem.at[d - 1], 2)
        tell(z_sem.at[d], along_z)
        prepare(2 * d - 1)
        send(2 * d - 1)
        pl.semaphore_wait(plane_sem.at[d - 1], 3)

        @pl.when(d < 3)
        def _():
            tell(plane_sem.at[d], bands)

        prepare(2 * d)
        send(2 * d)
        return c

    lax.fori_loop(1, 4, ring, 0)
    pl.semaphore_wait(z_sem.at[3], 2)
    prepare(NZ - 1)
    for g in range(NX):
        valid_copy(z_at(NZ - 1) * NX + g).start()
        slab_copy(NZ - 1, g, first_rows, recv_sem.at[acq]).start()
    for g in range(NX):
        slab_copy(NZ - 1, g, last_rows, last_sem.at[x]).start()

    for a in range(ACQ - PARTNERS, ACQ):
        for part in range(2):
            at = part * PAIRS_Z + a % NX * PARTNERS
            sums[a // NX, at + ACQ - 1 - a : at + PARTNERS] = jnp.zeros(
                (a - ACQ + PARTNERS + 1, 8, 128), F32
            )
    sums[:, POWER_AT + NX :] = jnp.zeros((NZ, SUMS - POWER_AT - NX, 8, 128), F32)
    dense[SUMS:, :] = jnp.zeros((128 - SUMS, 128), F32)

    sublane = lax.broadcasted_iota(jnp.int32, (8, 128), 0)
    lane = lax.broadcasted_iota(jnp.int32, (8, 128), 1)
    upper = sublane < 4
    sign = jnp.where(upper, -1.0, 1.0).astype(F32)

    def slab_arrival(i, at, recv):
        return pltpu.make_async_remote_copy(
            src_ref=outgoing.at[0, at, :],
            dst_ref=arrived.at[i, at, :],
            send_sem=send_sem,
            recv_sem=recv,
            device_id=(acq, band),
            device_id_type=MESH,
        )

    all_valid[acq] = own_valid[...]

    def widen(i, begin, end):
        for t in range(begin // 8, end // 8):
            at = pl.ds(t * 8, 8)
            value = arrived[i, at, :].astype(F32)
            lead[i, at, :] = value
            turned[i, at, :] = pltpu.roll(value, 4, 0) * sign

    def pair_sums(za, gap, begin=0, end=SLAB):
        pairs = [
            (xa, xb)
            for xa in range(NX)
            for xb in range(NX)
            if 1 <= gap * NX + xb - xa <= PARTNERS
        ]
        powers = range(NX) if gap == 0 else ()

        def body(c, carry):
            carry = list(carry)
            for r in range(5):
                at = pl.ds(pl.multiple_of(c * 40 + r * 8, 8), 8)
                first = [lead[za * NX + i, at, :] for i in range(NX)]
                later = [lead[(za + gap) * NX + i, at, :] for i in range(NX)]
                later_turned = [turned[(za + gap) * NX + i, at, :] for i in range(NX)]
                m = 0
                for xa, xb in pairs:
                    carry[m] = carry[m] + first[xa] * later[xb]
                    carry[m + 1] = carry[m + 1] + first[xa] * later_turned[xb]
                    m += 2
                for i in powers:
                    carry[m] = carry[m] + first[i] * first[i]
                    m += 1
            return tuple(carry)

        slots = []
        for xa, xb in pairs:
            slot = xa * PARTNERS + gap * NX + xb - xa - 1
            slots += [slot, PAIRS_Z + slot]
        slots += [POWER_AT + i for i in powers]
        if begin:
            total = tuple(sums[za, slot] for slot in slots)
        else:
            total = (jnp.zeros((8, 128), F32),) * len(slots)
        total = lax.fori_loop(begin // 40, end // 40, body, total)
        for slot, value in zip(slots, total):
            sums[za, slot] = value

    def plane_sums(step, begin=0, end=SLAB):
        zn = z_at(step)
        pair_sums(zn, 0, begin, end)
        for gap in (1, 2, 3):

            def side(s, c):
                za = jnp.where(s == 0, zn - gap, zn)
                other = jnp.where(s == 0, zn - gap, zn + gap)
                place = z_position(lax.rem(other - z + 2 * NZ, NZ))

                @pl.when((other >= 0) & (other < NZ) & (place < step))
                def _():
                    pair_sums(za, gap, begin, end)

                return c

            lax.fori_loop(0, 2, side, 0)

    def arrival(step, carry):
        for i in range(NX):
            source = z_at(step) * NX + i

            @pl.when(source != acq)
            def _():
                slab_arrival(source, whole, recv_sem.at[source]).wait_recv()

            @pl.when(source == acq)
            def _():
                self_copy.wait()

            widen(source, 0, SLAB)
        plane_sums(step)
        return carry

    def last_arrival():
        plane = z_at(NZ - 1) * NX
        for i in range(NX):
            slab_arrival(plane + i, first_rows, recv_sem.at[plane + i]).wait_recv()
            widen(plane + i, 0, CUT)
        plane_sums(NZ - 1, 0, CUT)
        for i in range(NX):
            slab_arrival(plane + i, last_rows, last_sem.at[i]).wait_recv()
            widen(plane + i, CUT, SLAB)
        plane_sums(NZ - 1, CUT, SLAB)

    top_lane = (lane & 64) == 0
    mid_lane = (lane & 32) == 0
    s1 = (sublane & 2) == 0
    s0 = (sublane & 1) == 0

    def gather_group(za, group):
        v = [sums[za, group * 8 + i] for i in range(8)]

        def fold_part(a, b):
            return jnp.where(upper, a, b) + pltpu.roll(jnp.where(upper, b, a), 4, 0)

        v = [fold_part(v[i], v[i + 4]) for i in range(4)]

        def fold_top(a, b):
            return jnp.where(top_lane, a, b) + pltpu.roll(jnp.where(top_lane, b, a), 64, 1)

        v = [fold_top(v[i], v[i + 2]) for i in range(2)]
        a, b = v
        w = jnp.where(mid_lane, a + pltpu.roll(a, 96, 1), b + pltpu.roll(b, 32, 1))
        u = pltpu.roll(w, 64, 1)
        w = jnp.where(
            s1 == top_lane, w, jnp.where(s1, pltpu.roll(u, 6, 0), pltpu.roll(u, 2, 0))
        )
        w = jnp.where(
            s0 == mid_lane,
            w,
            jnp.where(
                s0,
                pltpu.roll(pltpu.roll(w, 32, 1), 7, 0),
                pltpu.roll(pltpu.roll(w, 96, 1), 1, 0),
            ),
        )
        return w

    def fill_message(q):
        def half(i, c):
            za = lax.rem(z + 2 * q + i + NZ - 3, NZ)
            values = [gather_group(za, group) for group in range(SUMS // 8)]
            for group, value in enumerate(values):
                dense[group * 8 : group * 8 + 8, :] = value
            flipped = dense[...].T
            for lr in range(4):
                message[q, pl.ds(i * 4 + lr, 32, stride=8), :] = flipped[
                    lr * 32 : (lr + 1) * 32, :
                ]
            return c

        lax.fori_loop(0, 2, half, 0)

    own_look = x * 8 + band
    own_source = band * NX + x

    def message_rows(look):
        return pl.ds(pl.multiple_of(look * 8, 8), 8)

    def message_copy(q, look):
        return pltpu.make_async_remote_copy(
            src_ref=message.at[q, message_rows(look), :],
            dst_ref=received.at[q, own_source],
            send_sem=send2_sem.at[q],
            recv_sem=recv2_sem.at[q],
            device_id=(z * NX + look // 8, lax.rem(look, 8)),
            device_id_type=MESH,
        )

    def send_message(q):
        def one(s, c):
            message_copy(q, lax.rem(own_look + s, ACQ)).start()
            return c

        lax.fori_loop(1, ACQ, one, 0)
        received[q, own_source] = message[q, message_rows(own_look), :]

    lax.fori_loop(0, NZ - 1, arrival, 0)
    for q in (0, 1):
        fill_message(q)
        send_message(q)
    last_arrival()
    for q in (2, 3):
        fill_message(q)
        send_message(q)

    valid_group = all_valid.at[pl.ds(0, ACQ - 1)]
    pltpu.make_async_copy(valid_group, valid_group, vrecv_sem).wait()
    pltpu.make_async_copy(valid_group, valid_group, vsend_sem).wait()
    slab_group = outgoing.at[pl.ds(0, ACQ - 1)]
    pltpu.make_async_copy(slab_group, slab_group, send_sem).wait()

    valid = all_valid[...].reshape(ACQ, 128)
    by_partner = jnp.concatenate([valid, jnp.zeros((96, 128), F32)], axis=0).T
    partner = lax.broadcasted_iota(jnp.int32, (16, 128), 0)
    for a in range(ACQ):
        on = jnp.broadcast_to(by_partner[0:16, a : a + 1], (16, 128)) * (1.0 / CELLS)
        on = jnp.where(partner < ACQ - 1 - a, on, 0.0)
        weight[a * PARTNERS : a * PARTNERS + PARTNERS, :] = on[0:PARTNERS, :]

    for q in range(4):
        group = received.at[q, pl.ds(0, ACQ - 1)]
        pltpu.make_async_copy(group, group, recv2_sem.at[q]).wait()
        pltpu.make_async_copy(group, group, send2_sem.at[q]).wait()
        halves = [[], []]
        for s in range(0, ACQ, 2):
            a = received[q, s]
            b = received[q, s + 1]
            halves[0].append(jnp.where(upper, a, pltpu.roll(b, 4, 0)))
            halves[1].append(jnp.where(upper, pltpu.roll(a, 4, 0), b))
        for i in range(2):
            za = lax.rem(z + 2 * q + i + NZ - 3, NZ)
            final[za] = jnp.concatenate(halves[i], axis=0).T[0:SUMS, :]

    power[...] = jnp.ones_like(power)
    for za in range(NZ):
        power[za * NX : za * NX + NX, :] = (
            final[za, POWER_AT : POWER_AT + NX, :] * (1.0 / CELLS) + EPS
        )
    for a in range(ACQ):
        at = a * PARTNERS
        pair_power = power[a : a + 1, :] * power[a + 1 : a + 1 + PARTNERS, :]
        weight[at : at + PARTNERS, :] = weight[at : at + PARTNERS, :] * lax.rsqrt(pair_power)
    for za in range(NZ):
        at = za * PAIRS_Z
        scale = weight[at : at + PAIRS_Z, :]
        for part in range(2):
            out_ref[part, at : at + PAIRS_Z, :] = (
                final[za, part * PAIRS_Z : (part + 1) * PAIRS_Z, :] * scale
            )


def per_device(slc, validity):
    dma = pltpu.SemaphoreType.DMA
    out = pl.pallas_call(
        kernel,
        out_shape=jax.ShapeDtypeStruct((2, ACQ * PARTNERS, 128), F32),
        in_specs=[
            pl.BlockSpec(memory_space=pl.ANY),
            pl.BlockSpec(memory_space=pltpu.VMEM),
        ],
        out_specs=pl.BlockSpec(memory_space=pltpu.VMEM),
        scratch_shapes=[
            pltpu.VMEM((NZ, 2, 80, BLOCK), BF16),
            pltpu.VMEM((BLOCK, BLOCK), BF16),
            pltpu.VMEM((ACQ, SLAB, 128), BF16),
            pltpu.VMEM((ACQ, SLAB, 128), BF16),
            pltpu.VMEM((ACQ, SLAB, 128), F32),
            pltpu.VMEM((ACQ, SLAB, 128), F32),
            pltpu.VMEM((NZ, SUMS, 8, 128), F32),
            pltpu.VMEM((128, 128), F32),
            pltpu.VMEM((4, 256, 128), F32),
            pltpu.VMEM((4, ACQ, 8, 128), F32),
            pltpu.VMEM((NZ, SUMS, 128), F32),
            pltpu.VMEM((ACQ * PARTNERS, 128), F32),
            pltpu.VMEM((1, 128), F32),
            pltpu.VMEM((ACQ, 1, 128), F32),
            pltpu.VMEM((48, 128), F32),
            pltpu.SemaphoreType.REGULAR((4,)),
            pltpu.SemaphoreType.REGULAR((3,)),
            dma((NZ,)),
            dma,
            dma,
            dma((ACQ,)),
            dma((NX,)),
            dma,
            dma,
            dma((4,)),
            dma((4,)),
        ],
        compiler_params=pltpu.CompilerParams(
            collective_id=0, has_side_effects=True, vmem_limit_bytes=56 * 2**20
        ),
    )(slc, validity)
    return out.transpose(0, 2, 1)[:, :, None, :]


def solution(mesh):
    in_specs = (P(None, "acq", "rows", None), P("acq", None))
    out_specs = P(None, None, ("acq", "rows"), None)
    return jax.shard_map(
        per_device, mesh=mesh, in_specs=in_specs, out_specs=out_specs, check_vma=False
    )
```

```python
import jax
import jax.numpy as jnp
from jax import lax
from jax.sharding import PartitionSpec as P
from jax.experimental import pallas as pl
from jax.experimental.pallas import tpu as pltpu

PARTNERS = 10
EPS = 1e-06
CELLS = 100.0
ACQ = 32
NX = 4
NZ = 8
BLOCK = 640
CUT = 160
SLAB = 200
PAIRS_Z = NX * PARTNERS
POWER_AT = 2 * PAIRS_Z
SUMS = 88
MESH = pl.DeviceIdType.MESH
F32 = jnp.float32
BF16 = jnp.bfloat16


def z_offset(step):
    half = (step + 1) // 2
    return jnp.where(step % 2 == 1, half, lax.rem(NZ - half, NZ))


def z_position(offset):
    return jnp.where(offset <= 4, jnp.maximum(2 * offset - 1, 0), 2 * (NZ - offset))


def row_table():
    pieces = []
    for g in range(NX):
        q = lax.broadcasted_iota(jnp.int32, (40, 160), 0)
        take = ((q >> 2) & 1) * 80 + (4 * g + (q & 3)) * 5 + (q >> 3)
        pieces.append((lax.broadcasted_iota(jnp.int32, (40, 160), 1) == take).astype(F32))
    return jnp.concatenate(pieces, axis=0).astype(BF16)


def column_table():
    c = lax.broadcasted_iota(jnp.int32, (BLOCK, BLOCK), 1)
    take = (c & 31) * 20 + (c >> 7) * 4 + ((c >> 5) & 3)
    return (lax.broadcasted_iota(jnp.int32, (BLOCK, BLOCK), 0) == take).astype(F32).astype(BF16)


def kernel(
    slc_ref, validity_ref, out_ref,
    image, table, outgoing, arrived, lead, turned, sums, dense, message, received,
    final, weight, own_valid, all_valid, power,
    z_sem, plane_sem, in_sem, self_sem, send_sem, recv_sem, last_sem, vsend_sem, vrecv_sem, send2_sem, recv2_sem,
):
    acq = lax.axis_index("acq")
    band = lax.axis_index("rows")
    z = acq // NX
    x = lax.rem(acq, NX)

    def z_at(step):
        return lax.rem(z + z_offset(step), NZ)

    def load_block(n):
        at = pl.multiple_of(z_at(n) * BLOCK, 128)
        return pltpu.make_async_copy(
            slc_ref.at[:, 0, :, pl.ds(at, BLOCK)], image.at[n], in_sem.at[n]
        )

    for n in range(NZ):
        load_block(n).start()

    barrier = pltpu.get_barrier_semaphore()
    along_z = [(lax.rem(z + d, NZ) * NX + x, band) for d in (1, NZ - 1)]
    along_x = [(z * NX + lax.rem(x + d, NX), band) for d in (1, 2, 3)]
    bands = [(acq, lax.rem(band + d, 8)) for d in (2, 6)]
    bands.append((acq, band + 1 - 2 * lax.rem(band, 2)))

    def tell(semaphore, devices):
        for device in devices:
            pl.semaphore_signal(semaphore, inc=1, device_id=device, device_id_type=MESH)

    tell(barrier, along_x + along_z + bands)

    own_valid[...] = jnp.zeros_like(own_valid)
    own_valid[:, 0:PARTNERS] = (validity_ref[...] > 0).astype(F32)
    rows = row_table()
    table[...] = column_table()

    def prepare(n):
        load_block(n).wait()
        block = image[n].reshape(160, BLOCK)
        ordered = jnp.dot(rows, block, preferred_element_type=F32).astype(BF16)
        slab = jnp.dot(ordered, table[...], preferred_element_type=F32).astype(BF16)
        for g in range(NX):
            for c in range(5):
                outgoing[n * NX + g, c * 40 : (c + 1) * 40, :] = slab[
                    g * 40 : (g + 1) * 40, c * 128 : (c + 1) * 128
                ]

    def slab_copy(n, g, at, recv):
        return pltpu.make_async_remote_copy(
            src_ref=outgoing.at[n * NX + g, at, :],
            dst_ref=arrived.at[acq, at, :],
            send_sem=send_sem,
            recv_sem=recv,
            device_id=(z_at(n) * NX + g, band),
            device_id_type=MESH,
        )

    whole = pl.ds(0, SLAB)
    first_rows = pl.ds(0, CUT)
    last_rows = pl.ds(CUT, SLAB - CUT)

    def valid_copy(to):
        return pltpu.make_async_remote_copy(
            src_ref=own_valid,
            dst_ref=all_valid.at[acq],
            send_sem=vsend_sem,
            recv_sem=vrecv_sem,
            device_id=(to, band),
            device_id_type=MESH,
        )

    self_copy = pltpu.make_async_copy(outgoing.at[x], arrived.at[acq], self_sem)

    def send(n):
        for g in range(NX):
            to = z_at(n) * NX + g

            @pl.when(to != acq)
            def _():
                valid_copy(to).start()
                slab_copy(n, g, whole, recv_sem.at[acq]).start()

    prepare(0)
    pl.semaphore_wait(barrier, 8)
    tell(z_sem.at[0], along_z)
    tell(plane_sem.at[0], bands)
    send(0)
    self_copy.start()

    def ring(d, c):
        pl.semaphore_wait(z_sem.at[d - 1], 2)
        tell(z_sem.at[d], along_z)
        prepare(2 * d - 1)
        send(2 * d - 1)
        pl.semaphore_wait(plane_sem.at[d - 1], 3)

        @pl.when(d < 3)
        def _():
            tell(plane_sem.at[d], bands)

        prepare(2 * d)
        send(2 * d)
        return c

    lax.fori_loop(1, 4, ring, 0)
    pl.semaphore_wait(z_sem.at[3], 2)
    prepare(NZ - 1)
    for g in range(NX):
        valid_copy(z_at(NZ - 1) * NX + g).start()
        slab_copy(NZ - 1, g, first_rows, recv_sem.at[acq]).start()
    for g in range(NX):
        slab_copy(NZ - 1, g, last_rows, last_sem.at[x]).start()

    for a in range(ACQ - PARTNERS, ACQ):
        for part in range(2):
            at = part * PAIRS_Z + a % NX * PARTNERS
            sums[a // NX, at + ACQ - 1 - a : at + PARTNERS] = jnp.zeros(
                (a - ACQ + PARTNERS + 1, 8, 128), F32
            )
    sums[:, POWER_AT + NX :] = jnp.zeros((NZ, SUMS - POWER_AT - NX, 8, 128), F32)
    dense[NZ * SUMS :, :] = jnp.zeros((768 - NZ * SUMS, 128), F32)

    sublane = lax.broadcasted_iota(jnp.int32, (8, 128), 0)
    lane = lax.broadcasted_iota(jnp.int32, (8, 128), 1)
    upper = sublane < 4
    sign = jnp.where(upper, -1.0, 1.0).astype(F32)

    def slab_arrival(i, at, recv):
        return pltpu.make_async_remote_copy(
            src_ref=outgoing.at[0, at, :],
            dst_ref=arrived.at[i, at, :],
            send_sem=send_sem,
            recv_sem=recv,
            device_id=(acq, band),
            device_id_type=MESH,
        )

    all_valid[acq] = own_valid[...]

    def widen(i, begin, end):
        for t in range(begin // 8, end // 8):
            at = pl.ds(t * 8, 8)
            value = arrived[i, at, :].astype(F32)
            lead[i, at, :] = value
            turned[i, at, :] = pltpu.roll(value, 4, 0) * sign

    def pair_sums(za, gap, begin=0, end=SLAB):
        pairs = [
            (xa, xb)
            for xa in range(NX)
            for xb in range(NX)
            if 1 <= gap * NX + xb - xa <= PARTNERS
        ]
        powers = range(NX) if gap == 0 else ()

        def body(c, carry):
            carry = list(carry)
            for r in range(5):
                at = pl.ds(pl.multiple_of(c * 40 + r * 8, 8), 8)
                first = [lead[za * NX + i, at, :] for i in range(NX)]
                later = [lead[(za + gap) * NX + i, at, :] for i in range(NX)]
                later_turned = [turned[(za + gap) * NX + i, at, :] for i in range(NX)]
                m = 0
                for xa, xb in pairs:
                    carry[m] = carry[m] + first[xa] * later[xb]
                    carry[m + 1] = carry[m + 1] + first[xa] * later_turned[xb]
                    m += 2
                for i in powers:
                    carry[m] = carry[m] + first[i] * first[i]
                    m += 1
            return tuple(carry)

        slots = []
        for xa, xb in pairs:
            slot = xa * PARTNERS + gap * NX + xb - xa - 1
            slots += [slot, PAIRS_Z + slot]
        slots += [POWER_AT + i for i in powers]
        if begin:
            total = tuple(sums[za, slot] for slot in slots)
        else:
            total = (jnp.zeros((8, 128), F32),) * len(slots)
        total = lax.fori_loop(begin // 40, end // 40, body, total)
        for slot, value in zip(slots, total):
            sums[za, slot] = value

    def plane_sums(step, begin=0, end=SLAB):
        zn = z_at(step)
        pair_sums(zn, 0, begin, end)
        for gap in (1, 2, 3):

            def side(s, c):
                za = jnp.where(s == 0, zn - gap, zn)
                other = jnp.where(s == 0, zn - gap, zn + gap)
                place = z_position(lax.rem(other - z + 2 * NZ, NZ))

                @pl.when((other >= 0) & (other < NZ) & (place < step))
                def _():
                    pair_sums(za, gap, begin, end)

                return c

            lax.fori_loop(0, 2, side, 0)

    def arrival(step, carry):
        for i in range(NX):
            source = z_at(step) * NX + i

            @pl.when(source != acq)
            def _():
                slab_arrival(source, whole, recv_sem.at[source]).wait_recv()

            @pl.when(source == acq)
            def _():
                self_copy.wait()

            widen(source, 0, SLAB)
        plane_sums(step)
        return carry

    def last_arrival():
        plane = z_at(NZ - 1) * NX
        for i in range(NX):
            slab_arrival(plane + i, first_rows, recv_sem.at[plane + i]).wait_recv()
            widen(plane + i, 0, CUT)
        plane_sums(NZ - 1, 0, CUT)
        for i in range(NX):
            slab_arrival(plane + i, last_rows, last_sem.at[i]).wait_recv()
            widen(plane + i, CUT, SLAB)
        plane_sums(NZ - 1, CUT, SLAB)

    top_lane = (lane & 64) == 0
    mid_lane = (lane & 32) == 0
    s1 = (sublane & 2) == 0
    s0 = (sublane & 1) == 0

    def gather_group(za, group):
        v = [sums[za, group * 8 + i] for i in range(8)]

        def fold_part(a, b):
            return jnp.where(upper, a, b) + pltpu.roll(jnp.where(upper, b, a), 4, 0)

        v = [fold_part(v[i], v[i + 4]) for i in range(4)]

        def fold_top(a, b):
            return jnp.where(top_lane, a, b) + pltpu.roll(jnp.where(top_lane, b, a), 64, 1)

        v = [fold_top(v[i], v[i + 2]) for i in range(2)]
        a, b = v
        w = jnp.where(mid_lane, a + pltpu.roll(a, 96, 1), b + pltpu.roll(b, 32, 1))
        u = pltpu.roll(w, 64, 1)
        w = jnp.where(
            s1 == top_lane, w, jnp.where(s1, pltpu.roll(u, 6, 0), pltpu.roll(u, 2, 0))
        )
        w = jnp.where(
            s0 == mid_lane,
            w,
            jnp.where(
                s0,
                pltpu.roll(pltpu.roll(w, 32, 1), 7, 0),
                pltpu.roll(pltpu.roll(w, 96, 1), 1, 0),
            ),
        )
        return w

    def gather(i, c):
        za = lax.rem(z + i + NZ - 3, NZ)
        values = [gather_group(za, group) for group in range(SUMS // 8)]
        for group, value in enumerate(values):
            dense[pl.ds(pl.multiple_of(i * SUMS + group * 8, 8), 8), :] = value
        return c

    def fill_message(tile):
        flipped = dense[tile * 128 : tile * 128 + 128, :].T
        for lr in range(4):
            message[tile // 2, pl.ds(tile % 2 * 4 + lr, 32, stride=8), :] = flipped[
                lr * 32 : (lr + 1) * 32, :
            ]

    own_look = x * 8 + band
    own_source = band * NX + x

    def message_rows(look):
        return pl.ds(pl.multiple_of(look * 8, 8), 8)

    def message_copy(look):
        return pltpu.make_async_remote_copy(
            src_ref=message.at[:, message_rows(look), :],
            dst_ref=received.at[:, own_source],
            send_sem=send2_sem,
            recv_sem=recv2_sem,
            device_id=(z * NX + look // 8, lax.rem(look, 8)),
            device_id_type=MESH,
        )

    def send_message(s, c):
        message_copy(lax.rem(own_look + s, ACQ)).start()
        return c

    lax.fori_loop(0, NZ - 1, arrival, 0)
    lax.fori_loop(0, 4, gather, 0)
    fill_message(0)
    fill_message(1)
    last_arrival()
    lax.fori_loop(4, NZ, gather, 0)
    for tile in range(2, 6):
        fill_message(tile)
    lax.fori_loop(1, ACQ, send_message, 0)
    for h in range(3):
        received[h, own_source] = message[h, message_rows(own_look), :]

    valid_group = all_valid.at[pl.ds(0, ACQ - 1)]
    pltpu.make_async_copy(valid_group, valid_group, vrecv_sem).wait()
    pltpu.make_async_copy(valid_group, valid_group, vsend_sem).wait()
    slab_group = outgoing.at[pl.ds(0, ACQ - 1)]
    pltpu.make_async_copy(slab_group, slab_group, send_sem).wait()

    valid = all_valid[...].reshape(ACQ, 128)
    by_partner = jnp.concatenate([valid, jnp.zeros((96, 128), F32)], axis=0).T
    partner = lax.broadcasted_iota(jnp.int32, (16, 128), 0)
    for a in range(ACQ):
        on = jnp.broadcast_to(by_partner[0:16, a : a + 1], (16, 128)) * (1.0 / CELLS)
        on = jnp.where(partner < ACQ - 1 - a, on, 0.0)
        weight[a * PARTNERS : a * PARTNERS + PARTNERS, :] = on[0:PARTNERS, :]

    group = received.at[:, pl.ds(0, ACQ - 1)]
    pltpu.make_async_copy(group, group, recv2_sem).wait()
    pltpu.make_async_copy(group, group, send2_sem).wait()
    for h in range(3):
        halves = [[], []]
        for s in range(0, ACQ, 2):
            a = received[h, s]
            b = received[h, s + 1]
            halves[0].append(jnp.where(upper, a, pltpu.roll(b, 4, 0)))
            halves[1].append(jnp.where(upper, pltpu.roll(a, 4, 0), b))
        for i in range(2):
            dense[h * 256 + i * 128 : h * 256 + i * 128 + 128, :] = jnp.concatenate(
                halves[i], axis=0
            ).T
    for i in range(NZ):
        final[lax.rem(z + i + NZ - 3, NZ)] = dense[i * SUMS : (i + 1) * SUMS, :]

    power[...] = jnp.ones_like(power)
    for za in range(NZ):
        power[za * NX : za * NX + NX, :] = (
            final[za, POWER_AT : POWER_AT + NX, :] * (1.0 / CELLS) + EPS
        )
    for a in range(ACQ):
        at = a * PARTNERS
        pair_power = power[a : a + 1, :] * power[a + 1 : a + 1 + PARTNERS, :]
        weight[at : at + PARTNERS, :] = weight[at : at + PARTNERS, :] * lax.rsqrt(pair_power)
    for za in range(NZ):
        at = za * PAIRS_Z
        scale = weight[at : at + PAIRS_Z, :]
        for part in range(2):
            out_ref[part, at : at + PAIRS_Z, :] = (
                final[za, part * PAIRS_Z : (part + 1) * PAIRS_Z, :] * scale
            )


def per_device(slc, validity):
    dma = pltpu.SemaphoreType.DMA
    out = pl.pallas_call(
        kernel,
        out_shape=jax.ShapeDtypeStruct((2, ACQ * PARTNERS, 128), F32),
        in_specs=[
            pl.BlockSpec(memory_space=pl.ANY),
            pl.BlockSpec(memory_space=pltpu.VMEM),
        ],
        out_specs=pl.BlockSpec(memory_space=pltpu.VMEM),
        scratch_shapes=[
            pltpu.VMEM((NZ, 2, 80, BLOCK), BF16),
            pltpu.VMEM((BLOCK, BLOCK), BF16),
            pltpu.VMEM((ACQ, SLAB, 128), BF16),
            pltpu.VMEM((ACQ, SLAB, 128), BF16),
            pltpu.VMEM((ACQ, SLAB, 128), F32),
            pltpu.VMEM((ACQ, SLAB, 128), F32),
            pltpu.VMEM((NZ, SUMS, 8, 128), F32),
            pltpu.VMEM((768, 128), F32),
            pltpu.VMEM((3, 256, 128), F32),
            pltpu.VMEM((3, ACQ, 8, 128), F32),
            pltpu.VMEM((NZ, SUMS, 128), F32),
            pltpu.VMEM((ACQ * PARTNERS, 128), F32),
            pltpu.VMEM((1, 128), F32),
            pltpu.VMEM((ACQ, 1, 128), F32),
            pltpu.VMEM((48, 128), F32),
            pltpu.SemaphoreType.REGULAR((4,)),
            pltpu.SemaphoreType.REGULAR((3,)),
            dma((NZ,)),
            dma,
            dma,
            dma((ACQ,)),
            dma((NX,)),
            dma,
            dma,
            dma,
            dma,
        ],
        compiler_params=pltpu.CompilerParams(
            collective_id=0, has_side_effects=True, vmem_limit_bytes=56 * 2**20
        ),
    )(slc, validity)
    return out.transpose(0, 2, 1)[:, :, None, :]


def solution(mesh):
    in_specs = (P(None, "acq", "rows", None), P("acq", None))
    out_specs = P(None, None, ("acq", "rows"), None)
    return jax.shard_map(
        per_device, mesh=mesh, in_specs=in_specs, out_specs=out_specs, check_vma=False
    )
```
